256 devices in a mesh: row: 16 (over x, z_hi), col: 4 (over y), depth: 4 (over z_lo, core).
Axes of the slice: x: 4, y: 4, z: 8 (z_hi: 4, z_lo: 2; z = z_hi * 2 + z_lo), core: 2. Of those that a mesh axis runs over, the one named last changes fastest.
Arguments:
- activations: float32 [2048, 8192], P(('col', 'depth'), 'row'), may hold values from -0.13258252 to 0.13258252
- grad_output: float32 [2048, 16384], P('row', ('col', 'depth')), may hold values from -6 to 6
- up_weight: float32 [8192, 16384], P('row', ('col', 'depth')), may hold values from -0.0625 to 0.0625
Outputs:
- grad_input: float32 [2048, 8192], P(('col', 'depth'), 'row')
- grad_weight: float32 [8192, 16384], P('row', ('col', 'depth'))
The draws below stay inside these ranges and needn't reach their ends.
All inputs are finite; a program needn't handle non-finite values.
Results may differ from the reference program's by a relative error of at most 0.000075.
Values sent between devices are 32-bit elements; how exact they have to be, the bound alone decides.
No kernel may reach another device: no remote copies, remote signals or barrier semaphores. Data moves between devices by JAX's collectives and lax.ppermute only.
A program may use at most 64 MiB of HBM per device.

```python
import jax
import jax.numpy as jnp
from jax import lax

D = 8192
F = 16384
TOKENS = 2048


def with_spikes(result, own_key, source, target, shards_of, factor):
    def block_of(position):
        return (jnp.arange(result.shape[position]) // (result.shape[position] // shards_of)).reshape((-1,) + (1,) * (result.ndim - 1 - position))

    near = jax.random.permutation(own_key, shards_of)[block_of(target)]
    second = (block_of(target) + shards_of // 2) % shards_of
    return jnp.where((block_of(source) == near) | (block_of(source) == second), factor * result, result)


def block_scale(key, dims, cuts, low, high):
    gain, own = 1.0, jax.random.fold_in(key, 6)
    for axis_at, parts in cuts:
        steps = jnp.exp(jax.random.uniform(jax.random.fold_in(own, axis_at), (parts,), jnp.float32, low / len(cuts), high / len(cuts)))
        gain = gain * jnp.repeat(steps, dims[axis_at] // parts).reshape([-1 if axis == axis_at else 1 for axis in range(len(dims))])
    return gain


def bell_draw(key, extent, width, bound, cuts=(), dtype=jnp.bfloat16):
    values = jax.random.normal(key, extent, jnp.float32) * width
    if len(cuts) > 0:
        values = block_scale(key, extent, cuts, -0.22, 0.18) * values
    return jnp.clip(values, min=-bound, max=bound).astype(dtype)


def noise_with(stream_key, shape, spread, most, shards, heavy, held_as=jnp.bfloat16):
    result = spread * jax.random.normal(stream_key, shape, jnp.float32)
    if shards:
        result = result * block_scale(stream_key, shape, shards, -0.22, 0.18)
    return jnp.clip(with_spikes(result, jax.random.fold_in(stream_key, 3), *heavy), -most, most).astype(held_as)


def setup_inputs(seed: int = 0) -> dict:
    keys = jax.random.split(jax.random.key(seed), 4)
    return {
        "activations": bell_draw(keys[0], (TOKENS, D), (TOKENS ** -0.5), 0.13258252, ((0, 16), (1, 16)), jnp.float32),
        "grad_output": noise_with(keys[1], (TOKENS, F), 1.0, 6.0, ((0, 16), (1, 16)), (1, 0, 16, 2.0), jnp.float32),
        "up_weight": bell_draw(keys[2], (D, F), D ** -0.5, 0.0625, ((0, 16), (1, 16)), jnp.float32),
    }


def reference(activations, grad_output, up_weight):
    highest = lax.Precision.HIGHEST
    grad_input = jnp.dot(grad_output, up_weight.T, precision=highest, preferred_element_type=jnp.float32)
    grad_weight = jnp.dot(activations.T, grad_output, precision=highest, preferred_element_type=jnp.float32)
    return grad_input, grad_weight
```

```python
import jax
import jax.numpy as jnp
from jax import lax
from jax.experimental import pallas as pl
from jax.experimental.pallas import tpu as pltpu
from jax.sharding import PartitionSpec as P

AXES = ("row", "col", "depth")


def device_of(x, y, z, core):
    x, y, z = x % 4, y % 4, z % 8
    return ((x * 4 + z // 2) * 4 + y) * 4 + (z % 2) * 2 + core


def pairs(move):
    out = []
    for x in range(4):
        for y in range(4):
            for z in range(8):
                for core in range(2):
                    to = move(x, y, z, core)
                    if to is not None:
                        out.append((device_of(x, y, z, core), device_of(*to)))
    return out


def sign(core):
    return 1 - 2 * core


X_A = pairs(lambda x, y, z, c: (x + sign(c), y, z, c))
X_B = pairs(lambda x, y, z, c: (x - sign(c), y, z, c))
Y_A = pairs(lambda x, y, z, c: (x, y + sign(c), z, c))
Y_B = pairs(lambda x, y, z, c: (x, y - sign(c), z, c))
Z_A = pairs(lambda x, y, z, c: (x, y, z + 2 * sign(c), c))
Z_B = pairs(lambda x, y, z, c: (x, y, z - 2 * sign(c), c))
Z_LO = pairs(lambda x, y, z, c: (x, y, z ^ 1, c))
CORE = pairs(lambda x, y, z, c: (x, y, z, 1 - c))


def owner(z, near):
    return (z // 2 + near) % 2


def to_owner(near):
    return pairs(lambda x, y, z, c: (x, y, z, 1 - c) if c != owner(z, near) else None)


def owner_y(near, step):
    return pairs(lambda x, y, z, c: (x, y + step, z, c) if c == owner(z, near) else None)


def owner_z(near):
    return pairs(lambda x, y, z, c: (x, y, z ^ 1, c) if c == owner(z, near) else None)


def send(value, to):
    return lax.ppermute(value, AXES, to)


VMEM = pl.BlockSpec(memory_space=pltpu.VMEM)
SMEM = pl.BlockSpec(memory_space=pltpu.SMEM)


def local_call(kernel, out, args, aliases={}):
    return pl.pallas_call(
        kernel,
        out_shape=out,
        in_specs=[SMEM] + [VMEM] * (len(args) - 1),
        out_specs=jax.tree.map(lambda _: VMEM, out),
        input_output_aliases=aliases,
        cost_estimate=pl.CostEstimate(flops=0, bytes_accessed=4 << 20, transcendentals=0),
    )(*args)


def f32(*shape):
    return jax.ShapeDtypeStruct(shape, jnp.float32)


def join_kernel(place, b0, b1, b2, b3, out):
    for k, b in enumerate((b0, b1, b2, b3)):
        out[k * 128 : (k + 1) * 128] = b[...]


def feats_kernel(place, *refs):
    out = refs[-1]
    for k, piece in enumerate(refs[:-1]):
        for n in range(2):
            out[place[2 * k + n]] = piece[n]


def pair_kernel(place, mine0, mine1, got0, got1, s0, s1, s2, s3):
    for step, out in enumerate((s0, s1, s2, s3)):
        own, other = place[step], place[4 + step]
        out[place[8]] = mine0[own] + got0[other]
        out[place[9]] = mine1[own] + got1[other]


def ints(values):
    return jnp.stack([jnp.asarray(v, jnp.int32) for v in values])


def after(value, *others):
    return lax.optimization_barrier((value, *others))[0]


def shards(activations, grad_output, up_weight):
    row, y, depth = lax.axis_index("row"), lax.axis_index("col"), lax.axis_index("depth")
    x, z_hi, z_lo, core = row // 4, row % 4, depth // 2, depth % 2
    way = 1 - 2 * core
    offsets = (0, -way, way, 2)

    two = jnp.stack([activations, send(activations, Z_LO)])
    g0 = grad_output
    g1 = send(g0, Z_A)
    g2 = send(after(g0, g1), Z_B)
    g3 = send(after(g1, g2), Z_A)
    groups = []
    for g in (g0, g1, g2, g3):
        near = send(g, X_A)
        groups.append((g, near, send(g, X_B), send(near, X_A)))

    near = send(two, Y_A)
    four = [two, near, send(two, Y_B), send(near, Y_A)]

    def slot_of(offset, turn):
        offset = offset % 4
        return jnp.where(offset == 0, 0, jnp.where(offset == 2, 3, jnp.where(offset == (-turn) % 4, 1, 2)))

    at = []
    for other in range(2):
        turn = way * (1 - 2 * other)
        for o in (0, -turn, turn, 2):
            for n in range(2):
                source_x, source_z = y + o, (z_lo ^ n) * 2 + (core ^ other)
                at.append(slot_of(source_z - z_hi, way) * 4 + slot_of(source_x - x, way))
    feats = local_call(
        feats_kernel, f32(16, 128, 512), (ints(at), *four, *[send(f, CORE) for f in four])
    ).reshape(2048, 512)

    zero = jnp.zeros((1,), jnp.int32)
    joined = [local_call(join_kernel, f32(512, 1024), (zero, *group)) for group in groups]
    parts = [
        jnp.dot(g, up_weight.T, precision="high", preferred_element_type=jnp.float32).reshape(4, 128, 512)
        for g in joined
    ]
    grad_weight = sum(
        jnp.dot(feats[k * 512 : (k + 1) * 512].T, g, precision="high", preferred_element_type=jnp.float32)
        for k, g in enumerate(joined)
    )

    def reduce_pair(first, second, off_first, near):
        got = [send(parts[k], to_owner(near)) for k in ((second, first) if near else (first, second))]
        give_first = (((z_hi + off_first) % 4) // 2) ^ z_lo
        place = [slot_of(y + step - x, turn) for turn in (way, -way) for step in range(4)]
        both = local_call(
            pair_kernel,
            [f32(2, 128, 512)] * 4,
            (ints(place + [give_first, 1 - give_first]), parts[first], parts[second], *got),
        )
        total = both[0]
        for k in (1, 3, 2):
            total = total + send(both[k], owner_y(near, k))
        return total[0] + send(total[1], owner_z(near))

    odd = reduce_pair(1, 2, -way, 1)
    even = reduce_pair(0, 3, 0, 0)
    grad_input = jnp.where((z_hi + core) % 2 == 1, odd, even)
    return grad_input, grad_weight


def solution(mesh):
    return jax.shard_map(
        shards,
        mesh=mesh,
        in_specs=(
            P(("col", "depth"), "row"),
            P("row", ("col", "depth")),
            P("row", ("col", "depth")),
        ),
        out_specs=(P(("col", "depth"), "row"), P("row", ("col", "depth"))),
        check_vma=False,
    )
```

```python
import functools

import jax
import jax.numpy as jnp
import numpy as np
from jax import lax
from jax.experimental import pallas as pl
from jax.experimental.pallas import tpu as pltpu
from jax.sharding import PartitionSpec as P

AXES = ("row", "col", "depth")


def device_of(x, y, z, core):
    x, y, z = x % 4, y % 4, z % 8
    return ((x * 4 + z // 2) * 4 + y) * 4 + (z % 2) * 2 + core


def pairs(move):
    out = []
    for x in range(4):
        for y in range(4):
            for z in range(8):
                for core in range(2):
                    to = move(x, y, z, core)
                    if to is not None:
                        out.append((device_of(x, y, z, core), device_of(*to)))
    return out


def sign(core):
    return 1 - 2 * core


X_A = pairs(lambda x, y, z, c: (x + sign(c), y, z, c))
X_B = pairs(lambda x, y, z, c: (x - sign(c), y, z, c))
Y_A = pairs(lambda x, y, z, c: (x, y + sign(c), z, c))
Y_B = pairs(lambda x, y, z, c: (x, y - sign(c), z, c))
Z_A = pairs(lambda x, y, z, c: (x, y, z + 2 * sign(c), c))
Z_B = pairs(lambda x, y, z, c: (x, y, z - 2 * sign(c), c))
Z_LO = pairs(lambda x, y, z, c: (x, y, z ^ 1, c))
CORE = pairs(lambda x, y, z, c: (x, y, z, 1 - c))


def owner(z, near):
    return (z // 2 + near) % 2


def to_owner(near):
    return pairs(lambda x, y, z, c: (x, y, z, 1 - c) if c != owner(z, near) else None)


def owner_y(near, step):
    return pairs(lambda x, y, z, c: (x, y + step, z, c) if c == owner(z, near) else None)


def owner_z(near):
    return pairs(lambda x, y, z, c: (x, y, z ^ 1, c) if c == owner(z, near) else None)


def send(value, to):
    return lax.ppermute(value, AXES, to)


VMEM = pl.BlockSpec(memory_space=pltpu.VMEM)
SMEM = pl.BlockSpec(memory_space=pltpu.SMEM)
ANY = pl.BlockSpec(memory_space=pl.ANY)


def slot_of(offset, turn):
    offset = offset % 4
    return 0 if offset == 0 else 3 if offset == 2 else 1 if offset == -turn % 4 else 2


def places(x, y, z, core):
    z_hi, z_lo, way = z // 2, z % 2, 1 - 2 * core
    table = []
    for other in range(2):
        turn = way * (1 - 2 * other)
        for n in range(2):
            for o in (0, -turn, turn, 2):
                source_x, source_z = y + o, (z_lo ^ n) * 2 + (core ^ other)
                table.append(slot_of(source_z - z_hi, way) * 4 + slot_of(source_x - x, way))
    for off_first in (-way, 0):
        give_first = (((z_hi + off_first) % 4) // 2) ^ z_lo
        table += [slot_of(y + step - x, turn) for turn in (way, -way) for step in range(4)]
        table += [give_first, 1 - give_first]
    return table


def place_table():
    table = np.zeros((256, 36), np.int32)
    for x in range(4):
        for y in range(4):
            for z in range(8):
                for core in range(2):
                    table[device_of(x, y, z, core)] = places(x, y, z, core)
    return table


def local_call(kernel, out, args, in_specs, out_specs, scratch=(), aliases={}):
    return pl.pallas_call(
        kernel,
        out_shape=out,
        in_specs=in_specs,
        out_specs=out_specs,
        scratch_shapes=list(scratch),
        input_output_aliases=aliases,
        compiler_params=pltpu.CompilerParams(vmem_limit_bytes=12 << 20),
        cost_estimate=pl.CostEstimate(flops=0, bytes_accessed=4 << 20, transcendentals=0),
    )(*args)


def f32(*shape):
    return jax.ShapeDtypeStruct(shape, jnp.float32)


def join_kernel(first, *refs):
    blocks, out, sem = refs[:4], refs[-2], refs[-1]
    copies = [
        pltpu.make_async_copy(b, out.at[pl.ds(first + k * 128, 128)], sem.at[k]) for k, b in enumerate(blocks)
    ]
    for copy in copies:
        copy.start()
    for copy in copies:
        copy.wait()


def join(first, blocks, whole):
    args = (*blocks,) + (() if whole is None else (whole,))
    return local_call(
        functools.partial(join_kernel, first),
        f32(2048, 1024),
        args,
        [ANY] * len(args),
        ANY,
        [pltpu.SemaphoreType.DMA((4,))],
        {} if whole is None else {4: 0},
    )


def feats_kernel(place, p0, p1, p2, p3, out, sem):
    copies = [
        pltpu.make_async_copy(p.at[n], out.at[place[0, 4 * k + n]], sem.at[4 * k + n])
        for k, p in enumerate((p0, p1, p2, p3))
        for n in range(4)
    ]
    for copy in copies:
        copy.start()
    for copy in copies:
        copy.wait()


def pair_kernel(base, place, mine0, mine1, got0, got1, s0, s1, s2, s3):
    for step, out in enumerate((s0, s1, s2, s3)):
        own, other = place[0, base + step], place[0, base + 4 + step]
        out[place[0, base + 8]] = mine0[own] + got0[other]
        out[place[0, base + 9]] = mine1[own] + got1[other]


def after(value, *others):
    return lax.optimization_barrier((value, *others))[0]


def shards(activations, grad_output, up_weight):
    z_hi, core = lax.axis_index("row") % 4, lax.axis_index("depth") % 2
    place = lax.dynamic_slice(jnp.asarray(place_table()), (lax.axis_index(AXES), 0), (1, 36))

    g0 = grad_output
    g1 = send(g0, Z_A)
    g2 = send(after(g0, g1), Z_B)
    g3 = send(after(g1, g2), Z_A)
    groups = []
    for g in (g0, g1, g2, g3):
        near = send(g, X_A)
        groups.append((g, near, send(g, X_B), send(near, X_A)))

    near = send(activations, Y_A)
    four = jnp.stack([activations, near, send(activations, Y_B), send(near, Y_A)])
    more = send(after(four, g3), Z_LO)
    feats = local_call(
        feats_kernel,
        f32(16, 128, 512),
        (place, four, more, send(four, CORE), send(more, CORE)),
        [SMEM] + [ANY] * 4,
        ANY,
        [pltpu.SemaphoreType.DMA((16,))],
    ).reshape(2048, 512)

    joined = None
    parts = []
    for k, group in enumerate(groups):
        joined = join(k * 512, group, joined)
        part = jnp.dot(
            joined[k * 512 : (k + 1) * 512], up_weight.T, precision="high", preferred_element_type=jnp.float32
        )
        parts.append(part.reshape(4, 128, 512))

    def reduce_pair(first, second, base, near, meanwhile=()):
        got = [send(parts[k], to_owner(near)) for k in ((second, first) if near else (first, second))]
        both = local_call(
            functools.partial(pair_kernel, base),
            [f32(2, 128, 512)] * 4,
            (place, parts[first], parts[second], *got),
            [SMEM] + [VMEM] * 4,
            [VMEM] * 4,
        )
        sums = [send(both[k], owner_y(near, k)) for k in (1, 3, 2)]
        sums = lax.optimization_barrier((*sums, *meanwhile))
        total = both[0] + sums[0] + sums[1] + sums[2]
        return total[0] + send(total[1], owner_z(near))

    odd = reduce_pair(1, 2, 16, 1)
    grad_weight = jnp.dot(feats.T, joined, precision="high", preferred_element_type=jnp.float32)
    even = reduce_pair(0, 3, 26, 0, (grad_weight,))
    grad_input = jnp.where((z_hi + core) % 2 == 1, odd, even)
    return grad_input, grad_weight


def solution(mesh):
    return jax.shard_map(
        shards,
        mesh=mesh,
        in_specs=(
            P(("col", "depth"), "row"),
            P("row", ("col", "depth")),
            P("row", ("col", "depth")),
        ),
        out_specs=(P(("col", "depth"), "row"), P("row", ("col", "depth"))),
        check_vma=False,
    )
```
